512 devices in a mesh: ctx: 32 (over x, z_lo, core), tp: 16 (over y, z_hi).
Axes of the slice: x: 4, y: 4, z: 16 (z_hi: 4, z_lo: 4; z = z_hi * 4 + z_lo), core: 2. Of those that a mesh axis runs over, the one named last changes fastest.
Arguments:
- queries: bfloat16 [8192, 4096], P('ctx', 'tp'), may hold values from -6 to 6
- keys: bfloat16 [8192, 512], P('ctx'), may hold values from -6 to 6
- values: bfloat16 [8192, 512], P('ctx'), may hold values from -6 to 6
- out_weight: bfloat16 [4096, 8192], P('tp'), may hold values from -0.125 to 0.125
- storm_mask: int32 [64, 64], replicated, may hold values from 0 to 1, as said below
Outputs:
- mixed: bfloat16 [8192, 8192], P('ctx', 'tp')
The draws below stay inside these ranges and needn't reach their ends.
Inputs may be any that keep to these rules, and one draw needn't show every extreme that they name: storm_mask[i, j] is 0 where j > i and 1 where 0 <= i - j < 4.
All inputs are finite; a program needn't handle non-finite values.
Results may differ from the reference program's by a relative error of at most 0.019.
Values may be sent and summed in bfloat16 or wider, within the bound.
A program may use at most 64 MiB of HBM per device.

```python
import jax
import jax.numpy as jnp
from jax import lax

D = 8192
HEADS = 32
KV_HEADS = 4
HDIM = 128
BLOCK = 128
BAND = 4
SEQUENCE_TOKENS = 8192
NB = 64
HD = 4096
GQ = 8
KEY_VALUE_WIDTH = 512
N_TP = 16


def paired_draw(key):
    width = HEADS * HDIM
    narrow = KV_HEADS * HDIM
    first_key, second_key = jax.random.split(jax.random.fold_in(key, 11), 2)
    query = jnp.clip(jax.random.normal(first_key, (SEQUENCE_TOKENS, width), jnp.float32), -6.0, 6.0)
    keyed = jnp.clip(jax.random.normal(second_key, (SEQUENCE_TOKENS, narrow), jnp.float32), -6.0, 6.0)
    return (query, keyed)


def draw_queries(key, part):
    return paired_draw(key)[0].astype(jnp.bfloat16)


def draw_keys(key, part):
    return paired_draw(key)[1].astype(jnp.bfloat16)


def draw_storm_mask(key, part):
    coins = jax.random.randint(jax.random.fold_in(key, 29), (NB, NB), 0, 4) == 0
    later = jnp.arange(NB)[:, None]
    earlier = jnp.arange(NB)[None, :]
    near = (earlier <= later) & (later - earlier < BAND)
    distant = (earlier < later) & coins
    return (near | distant).astype(jnp.int32)


def raised(drawn, rng, source, target, parts, factor):
    def block_of(dim):
        return (jnp.arange(drawn.shape[dim]) // (drawn.shape[dim] // parts)).reshape((-1,) + (1,) * (drawn.ndim - 1 - dim))

    one_side = jax.random.permutation(rng, parts)[block_of(target)]
    second = (block_of(target) + parts // 2) % parts
    return jnp.where((block_of(source) == one_side) | (block_of(source) == second), factor * drawn, drawn)


def steps_of(rng, dims, shards, low, high):
    def one(axis_at, parts):
        heights = jax.random.uniform(jax.random.fold_in(jax.random.fold_in(rng, 6), axis_at), (parts,), jnp.float32, low / len(shards), high / len(shards))
        return jnp.repeat(jnp.exp(heights), dims[axis_at] // parts).reshape((-1,) + (1,) * (len(dims) - axis_at - 1))

    gain = one(*shards[0])
    for cut in shards[1:]:
        gain = gain * one(*cut)
    return gain


def noise(stream_key, shape, scale, limit, cuts=(), held_as=jnp.bfloat16):
    factor_of = steps_of(stream_key, shape, cuts, -0.22, 0.18) if cuts else 1.0
    result = jax.random.normal(stream_key, shape, jnp.float32) * scale * factor_of
    return jnp.minimum(jnp.maximum(result, -limit), limit).astype(held_as)


def heavy_noise(rng, extent, scale, bound, pieces, heavy, held_as=jnp.bfloat16):
    values = scale * jax.random.normal(rng, extent, jnp.float32)
    if pieces:
        values = values * steps_of(rng, extent, pieces, -0.22, 0.18)
    return jnp.clip(raised(values, jax.random.fold_in(rng, 3), *heavy), -bound, bound).astype(held_as)


def setup_inputs(seed: int = 0) -> dict:
    streams_of = jax.random.split(jax.random.key(seed), 6)
    queries = draw_queries(jax.random.fold_in(streams_of[5], 71), 0)
    keys = draw_keys(jax.random.fold_in(streams_of[5], 71), 0)
    values = noise(streams_of[2], (SEQUENCE_TOKENS, KEY_VALUE_WIDTH), 1.0, 6.0, ((0, 32),))
    out_weight = heavy_noise(streams_of[3], (HD, D), HD ** -0.5, 0.125, ((0, 16),), (0, 1, 16, 2.0))
    storm_mask = draw_storm_mask(jax.random.fold_in(streams_of[5], 71), 0)
    return {"queries": queries, "keys": keys, "values": values, "out_weight": out_weight, "storm_mask": storm_mask}


def reference(queries, keys, values, out_weight, storm_mask):
    length = queries.shape[0]
    scale = HDIM ** -0.5
    block_of = jnp.arange(length) // BLOCK
    allowed = storm_mask[block_of][:, block_of] == 1

    def heads_first(array, count):
        return array.reshape(length, count, HDIM).transpose(1, 0, 2)

    def one_head(operands):
        query, keyed, weighted_values = operands
        scores = jnp.dot(query, keyed.T, preferred_element_type=jnp.float32) * scale
        scores = jnp.where(allowed, scores, -1e30)
        peak = jnp.max(scores, axis=1, keepdims=True)
        weights = jnp.where(allowed, jnp.exp(scores - peak), 0.0)
        total = jnp.sum(weights, axis=1, keepdims=True)
        summed = jnp.dot(weights.astype(jnp.bfloat16), weighted_values, preferred_element_type=jnp.float32)
        return (summed / total).astype(jnp.bfloat16)

    keyed_all = jnp.repeat(heads_first(keys, KV_HEADS), GQ, axis=0)
    valued_all = jnp.repeat(heads_first(values, KV_HEADS), GQ, axis=0)
    attended = lax.map(one_head, (heads_first(queries, HEADS), keyed_all, valued_all))
    attended = attended.transpose(1, 0, 2).reshape(length, HEADS * HDIM)
    group = HEADS * HDIM // N_TP
    output_rows = jnp.zeros((length, D), jnp.float32)
    for number in range(N_TP):
        partial_value = jnp.dot(attended[:, number * group:(number + 1) * group], out_weight[number * group:(number + 1) * group], preferred_element_type=jnp.float32).astype(jnp.bfloat16)
        output_rows = output_rows + lax.optimization_barrier(partial_value).astype(jnp.float32)
    return output_rows.astype(jnp.bfloat16)
```

```python
import functools

import jax
import jax.numpy as jnp
from jax import lax
from jax.experimental import pallas as pl
from jax.experimental.pallas import tpu as pltpu
from jax.sharding import PartitionSpec as P

HDIM = 128
BLOCK = 128
MESH = pl.DeviceIdType.MESH
F32 = jnp.float32
BF16 = jnp.bfloat16
SCALE2 = HDIM ** (-0.5) * 1.4426950408889634
ORDER = ((0, 0), (-1, 0), (1, 0), (0, -1), (0, 1), (2, 0), (0, 2), (-1, -1), (-1, 1), (1, -1), (1, 1),
         (2, -1), (2, 1), (-1, 2), (1, 2), (2, 2))
KV_SENDS = 72
W_SLOTS = (10, 14)


def kernel(q_hbm, k_hbm, v_hbm, w_hbm, mask_ref, out_ref, qs, kv, wbuf, abuf, m_ref, acc_ref,
           ys2, ysp, ysm, yrel, yin, yacc, yown,
           local_sem, kv_send, kv_recv, kv_sib, w_send, wz_recv, wx_recv, wx_sib,
           a_send, a_recv, y_send, y_rel_recv, y_recv):
    ctx, tp = lax.axis_index("ctx"), lax.axis_index("tp")
    x, zl, core = ctx // 8, (ctx // 2) % 4, ctx % 2
    y, zh = tp // 4, tp % 4
    z = zh * 4 + zl

    def at_x(d):
        return (((x + d + 4) % 4) * 8 + zl * 2 + core, tp)

    def at_z(d):
        zz = (z + d + 16) % 16
        return (x * 8 + (zz % 4) * 2 + core, y * 4 + zz // 4)

    def at_y(d):
        return (ctx, ((y + d + 4) % 4) * 4 + zh)

    sibling = (x * 8 + zl * 2 + (1 - core), tp)
    devices = {"x+": at_x(1), "x-": at_x(-1), "z+": at_z(1), "z-": at_z(-1), "s": sibling,
               "y+": at_y(1), "y-": at_y(-1), "h+": at_z(4), "h-": at_z(-4), "f+": at_z(5), "f-": at_z(-5)}

    def remote(src, dst, ssem, rsem, to):
        return pltpu.make_async_remote_copy(src_ref=src, dst_ref=dst, send_sem=ssem, recv_sem=rsem,
                                            device_id=devices[to], device_id_type=MESH)

    def group_of(dx, dz):
        return ((x + dx + 4) % 4) * 4 + (zl + dz + 4) % 4

    own_group = x * 4 + zl

    local = []

    def load(src, dst):
        copy = pltpu.make_async_copy(src, dst, local_sem.at[len(local)])
        copy.start()
        local.append(copy)
        return copy

    head = pl.ds(pl.multiple_of(y * HDIM, HDIM), HDIM)
    own_kv = []
    for typ in range(2):
        rows = pl.ds(typ * BLOCK, BLOCK)
        own_kv.append((load(k_hbm.at[rows, head], kv.at[own_group, core * 2 + typ, 0]),
                       load(v_hbm.at[rows, head], kv.at[own_group, core * 2 + typ, 1])))
    q_loads = [load(q_hbm.at[pl.ds(b * BLOCK, BLOCK), pl.ds(h * HDIM, HDIM)], qs.at[b, pl.ds(h * HDIM, HDIM)])
               for b in range(2) for h in range(2)]

    def w_columns(yy, zz):
        return pl.ds(pl.multiple_of((yy * 4 + zz) * 512, 512), 512)

    w_loads = [load(w_hbm.at[:, w_columns(yy, zh)], wbuf.at[zh, yy]) for yy in range(4)]

    barrier = pltpu.get_barrier_semaphore()
    for device in devices.values():
        pl.semaphore_signal(barrier, inc=1, device_id=device, device_id_type=MESH)
    pl.semaphore_wait(barrier, len(devices))

    sends = []

    shift = {"x+": (-1, 0), "x-": (1, 0), "z+": (0, -1), "z-": (0, 1)}
    count = [0]

    def kv_ref(typ, dx, dz, part, which=None):
        ref = kv.at[group_of(dx, dz), (core if which is None else which) * 2 + typ]
        return ref if part is None else ref.at[part]

    def kv_forward(typ, dx, dz, part, to):
        number = count[0]
        count[0] += 1

        def copy():
            ref = kv_ref(typ, dx, dz, part)
            if to == "s":
                rsem = kv_sib.at[typ, dx % 4, dz % 4]
            else:
                sx, sz = shift[to]
                rsem = kv_recv.at[typ, (dx + sx) % 4, (dz + sz) % 4, part or 0]
            return remote(ref, ref, kv_send.at[number], rsem, to)

        copy().start()
        sends.append(lambda: copy().wait_send())

    def kv_handle(dx, dz):
        for typ in range(2):
            along = (dx, dz) if typ == 0 else (dz, dx)
            one, two = ("x", "z") if typ == 0 else ("z", "x")
            if (dx, dz) == (0, 0):
                for part in range(2):
                    own_kv[typ][part].wait()
            else:
                last = along[1] if along[1] != 0 else along[0]
                parts = (0, 1) if last == 2 else (None,)
                for part in parts:
                    ref = kv_ref(typ, dx, dz, part)
                    remote(ref, ref, kv_send.at[0], kv_recv.at[typ, dx % 4, dz % 4, part or 0], "s").wait_recv()
            if along[1] == 0:
                if along[0] == 0:
                    kv_forward(typ, dx, dz, None, one + "+")
                    kv_forward(typ, dx, dz, None, one + "-")
                elif along[0] == -1:
                    kv_forward(typ, dx, dz, 0, one + "+")
                elif along[0] == 1:
                    kv_forward(typ, dx, dz, 1, one + "-")
                kv_forward(typ, dx, dz, None, two + "+")
                kv_forward(typ, dx, dz, None, two + "-")
            elif along[1] == -1:
                kv_forward(typ, dx, dz, 0, two + "+")
            elif along[1] == 1:
                kv_forward(typ, dx, dz, 1, two + "-")
        for typ in range(2):
            kv_forward(typ, dx, dz, None, "s")

    row0 = pl.multiple_of(core * 128, 128)
    w_rows = {"all": pl.ds(row0, 128), "low": pl.ds(row0, 64), "high": pl.ds(pl.multiple_of(row0 + 64, 64), 64)}
    w_count = [0]

    def w_send_sem():
        w_count[0] += 1
        return w_send.at[w_count[0] - 1]

    def w_ref(dzh, dx, rows):
        return wbuf.at[(zh + dzh + 4) % 4, (x + dx + 4) % 4, w_rows[rows]]

    w_dirs = {"+": (1, "low", 0, 3), "-": (-1, "high", 2, 0)}
    w_sems = {}
    for name in w_dirs:
        w_sems[name] = (w_send_sem(), w_send_sem())

    def w_first(name):
        sign, far, slot, edge = w_dirs[name]

        @pl.when(zl == edge)
        def _():
            for part, (reach, rows, to) in enumerate(((1, "all", "z" + name), (2, far, "f" + name))):
                src = w_hbm.at[w_rows[rows], w_columns(x, (zh + sign * reach + 4) % 4)]
                remote(src, w_ref(0, 0, rows), w_sems[name][part], wz_recv.at[slot + part], to).start()

    def w_slot(name, k):
        sign, far, slot, edge = w_dirs[name]
        here = k if sign == 1 else 3 - k

        @pl.when(zl == here)
        def _():
            for part, (reach, rows) in enumerate(((1, "all"), (2, far))):
                ref = w_ref(-sign * reach, 0, rows)
                copy = remote(ref, ref, w_sems[name][part], wz_recv.at[slot + part], "z" + name)
                copy.wait_recv()
                if k < 3:
                    copy.start()

    def w_z_waits():
        for name in w_dirs:
            for part, rows in enumerate(("all", w_dirs[name][1])):
                ref = w_ref(1, 0, rows)
                copy = remote(ref, ref, w_sems[name][part], wz_recv.at[w_dirs[name][2] + part], "z" + name)
                copy.wait_send()

    def w_forward(dzh, dx, rows, to):
        ref = w_ref(dzh, dx, rows)
        if to == "s":
            rsem = wx_sib.at[dzh % 4, dx % 4]
        else:
            sx = shift[to][0]
            rsem = wx_recv.at[dzh % 4, (dx + sx) % 4, 1 if rows == "high" else 0]
        copy = remote(ref, ref, w_send_sem(), rsem, to)
        copy.start()
        sends.append(lambda: copy.wait_send())

    def w_wait(dzh, dx, rows):
        ref = w_ref(dzh, dx, rows)
        remote(ref, ref, w_send.at[0], wx_recv.at[dzh % 4, dx % 4, 1 if rows == "high" else 0], "s").wait_recv()

    zhs = (-1, 1, 2)

    def w_x1():
        for dzh in zhs:
            w_forward(dzh, 0, "all", "x+")
            w_forward(dzh, 0, "all", "x-")
        for dzh in zhs:
            w_forward(dzh, 0, "all", "s")

    def w_x2():
        for dzh in zhs:
            w_wait(dzh, -1, "all")
            w_forward(dzh, -1, "low", "x+")
            w_wait(dzh, 1, "all")
            w_forward(dzh, 1, "high", "x-")
            w_forward(dzh, -1, "all", "s")
            w_forward(dzh, 1, "all", "s")

    def w_x3():
        for dzh in zhs:
            w_wait(dzh, 2, "low")
            w_wait(dzh, 2, "high")
            w_forward(dzh, 2, "all", "s")

    other_rows = pl.ds(pl.multiple_of((1 - core) * 128, 128), 128)

    def w_x4():
        for dzh in zhs:
            for dx in (0, -1, 1, 2):
                ref = wbuf.at[(zh + dzh + 4) % 4, (x + dx + 4) % 4, other_rows]
                remote(ref, ref, w_send.at[0], wx_sib.at[dzh % 4, dx % 4], "s").wait_recv()

    m_ref[...] = jnp.full(m_ref.shape, -1e30, F32)
    acc_ref[...] = jnp.zeros(acc_ref.shape, F32)
    for copy in q_loads:
        copy.wait()
    ones = jnp.ones((512, HDIM), BF16)

    def attend(group):
        keys = kv[group, :, 0].reshape(512, HDIM)
        values = jnp.concatenate([kv[group, :, 1].reshape(512, HDIM), ones], axis=1)
        for b in range(2):
            scores = lax.dot_general(qs[b], keys, (((1,), (1,)), ((), ())), preferred_element_type=F32)
            parts = []
            for j in range(4):
                allowed = mask_ref[ctx * 2 + b, group * 4 + j].astype(F32)
                parts.append(scores[:, j * BLOCK:(j + 1) * BLOCK] * SCALE2 + (allowed - 1.0) * 1e30)
            top = jnp.maximum(jnp.maximum(parts[0], parts[1]), jnp.maximum(parts[2], parts[3]))
            old = m_ref[b]
            new = jnp.maximum(old, jnp.max(top, axis=1, keepdims=True))
            factor = jnp.exp2(old - new)
            weights = jnp.concatenate([jnp.exp2(part - new).astype(BF16) for part in parts], axis=1)
            m_ref[b] = new
            acc_ref[b] = acc_ref[b] * jnp.concatenate([factor, factor], axis=1) + jnp.dot(
                weights, values, preferred_element_type=F32)

    def pick(number, axis):
        value = 0
        for e, offset in enumerate(ORDER):
            if offset[axis] % 4:
                value = value + jnp.where(number == e, offset[axis] % 4, 0)
        return value

    def step(i, carry):
        for e, (dx, dz) in enumerate(ORDER):
            @pl.when(i == e)
            def _():
                kv_handle(dx, dz)
                if e == 0:
                    w_first("+")
                    w_first("-")
                for k, slot in enumerate(W_SLOTS):
                    if slot == e:
                        w_slot("+", k)
                        w_slot("-", k)

        @pl.when(i > 0)
        def _():
            dx, dz = pick(i - 1, 0), pick(i - 1, 1)
            group = ((x + dx) % 4) * 4 + (zl + dz) % 4
            for typ in range(2):
                ref = kv.at[group, (1 - core) * 2 + typ]
                remote(ref, ref, kv_send.at[0], kv_sib.at[typ, dx, dz], "s").wait_recv()

            @pl.when(group <= own_group)
            def _():
                attend(group)
        return carry

    lax.fori_loop(0, len(ORDER) + 1, step, 0)

    a_count = [0]

    def a_ref(dzh, b, part):
        ref = abuf.at[(zh + dzh + 4) % 4, b]
        return ref if part is None else ref.at[pl.ds(part * 64, 64)]

    def a_forward(dzh, b, part, to):
        ref = a_ref(dzh, b, part)
        there = dzh - 1 if to == "h+" else dzh + 1
        copy = remote(ref, ref, a_send.at[a_count[0]], a_recv.at[b, there % 4, part or 0], to)
        a_count[0] += 1
        copy.start()
        sends.append(lambda: copy.wait_send())

    def a_wait(dzh, b, part):
        ref = a_ref(dzh, b, part)
        remote(ref, ref, a_send.at[0], a_recv.at[b, dzh % 4, part or 0], "s").wait_recv()

    for b in range(2):
        done = (acc_ref[b, :, :HDIM] / acc_ref[b, :, HDIM:]).astype(BF16)
        abuf[zh, b] = jnp.concatenate([done[:BLOCK], done[BLOCK:]], axis=1)
        a_forward(0, b, None, "h+")
        a_forward(0, b, None, "h-")

    for k in range(len(W_SLOTS), 4):
        w_slot("+", k)
        w_slot("-", k)
    w_x1()
    for b in range(2):
        a_wait(-1, b, None)
        a_forward(-1, b, 0, "h+")
        a_wait(1, b, None)
        a_forward(1, b, 1, "h-")
    w_x2()
    w_x3()
    w_x4()
    for copy in w_loads:
        copy.wait()

    y_count = [0]

    def y_forward(src, dst, rsem, to):
        copy = remote(src, dst, y_send.at[y_count[0]], rsem, to)
        y_count[0] += 1
        copy.start()
        sends.append(lambda: copy.wait_send())

    def project(b, dy):
        yy = (y + dy + 4) % 4
        total = jnp.dot(abuf[0, b], wbuf[0, yy], preferred_element_type=F32)
        for zz in range(1, 4):
            total = total + jnp.dot(abuf[zz, b], wbuf[zz, yy], preferred_element_type=F32)
        return total

    for b in range(2):
        a_wait(2, b, 0)
        a_wait(2, b, 1)
        far = project(b, 2).astype(BF16)
        for half in range(2):
            ys2[b, half] = far[:, half * 256:(half + 1) * 256]
            y_forward(ys2.at[b, half], yrel.at[b, half], y_rel_recv.at[b, half], "y+" if half == 0 else "y-")
        up = project(b, 1)
        ysp[b, 1] = up[:, 256:].astype(BF16)
        yacc[b, 0] = up[:, :256]
        y_forward(ysp.at[b, 1], yin.at[b, 0, 1], y_recv.at[b, 0, 1], "y+")
        down = project(b, -1)
        ysm[b, 0] = down[:, :256].astype(BF16)
        yacc[b, 1] = down[:, 256:]
        y_forward(ysm.at[b, 0], yin.at[b, 1, 0], y_recv.at[b, 1, 0], "y-")
        yown[b] = project(b, 0)
    for b in range(2):
        for half, sent, to in ((0, ysp, "y+"), (1, ysm, "y-")):
            remote(ys2.at[b, half], yrel.at[b, half], y_send.at[0], y_rel_recv.at[b, half], to).wait_recv()
            sent[b, half] = (yacc[b, half] + yrel[b, half].astype(F32)).astype(BF16)
            y_forward(sent.at[b, half], yin.at[b, half, half], y_recv.at[b, half, half], to)
    for b in range(2):
        for half in range(2):
            for side in range(2):
                remote(ys2.at[b, half], yin.at[b, side, half], y_send.at[0], y_recv.at[b, side, half], "s").wait_recv()
            columns = pl.ds(half * 256, 256)
            out_ref[pl.ds(b * BLOCK, BLOCK), columns] = (
                yown[b, :, columns] + yin[b, 0, half].astype(F32) + yin[b, 1, half].astype(F32)).astype(BF16)

    for wait in sends:
        wait()
    w_z_waits()


def body(queries, keys, values, out_weight, storm_mask):
    rows, width = queries.shape
    anywhere = pl.BlockSpec(memory_space=pl.ANY)
    dma = pltpu.SemaphoreType.DMA
    return pl.pallas_call(
        kernel,
        out_shape=jax.ShapeDtypeStruct((rows, 512), BF16),
        in_specs=[anywhere, anywhere, anywhere, anywhere, pl.BlockSpec(memory_space=pltpu.SMEM)],
        out_specs=pl.BlockSpec(memory_space=pltpu.VMEM),
        scratch_shapes=[
            pltpu.VMEM((2, 256, HDIM), BF16),
            pltpu.VMEM((16, 4, 2, BLOCK, HDIM), BF16),
            pltpu.VMEM((4, 4, 256, 512), BF16),
            pltpu.VMEM((4, 2, BLOCK, 256), BF16),
            pltpu.VMEM((2, 256, HDIM), F32),
            pltpu.VMEM((2, 256, 256), F32),
            pltpu.VMEM((2, 2, BLOCK, 256), BF16),
            pltpu.VMEM((2, 2, BLOCK, 256), BF16),
            pltpu.VMEM((2, 2, BLOCK, 256), BF16),
            pltpu.VMEM((2, 2, BLOCK, 256), BF16),
            pltpu.VMEM((2, 2, 2, BLOCK, 256), BF16),
            pltpu.VMEM((2, 2, BLOCK, 256), F32),
            pltpu.VMEM((2, BLOCK, 512), F32),
            dma((12,)), dma((KV_SENDS,)), dma((2, 4, 4, 2)), dma((2, 4, 4)),
            dma((28,)), dma((4,)), dma((4, 4, 2)), dma((4, 4)),
            dma((8,)), dma((2, 4, 2)), dma((12,)), dma((2, 2)), dma((2, 2, 2)),
        ],
        compiler_params=pltpu.CompilerParams(
            collective_id=0, has_side_effects=True, vmem_limit_bytes=56 * 1024 * 1024),
    )(queries, keys, values, out_weight, storm_mask)


def solution(mesh):
    placed = (P("ctx", "tp"), P("ctx", None), P("ctx", None), P("tp", None), P())
    return jax.shard_map(
        body, mesh=mesh, in_specs=placed, out_specs=P("ctx", "tp"), check_vma=False
    )
```

```python
import functools

import jax
import jax.numpy as jnp
from jax import lax
from jax.experimental import pallas as pl
from jax.experimental.pallas import tpu as pltpu
from jax.sharding import PartitionSpec as P

HDIM = 128
BLOCK = 128
MESH = pl.DeviceIdType.MESH
F32 = jnp.float32
BF16 = jnp.bfloat16
SCALE2 = HDIM ** (-0.5) * 1.4426950408889634
PROGRAM = (
    ((0, 0), ()),
    ((0, -1), ((0, -1, 0), (0, 1, 0), (0, 0, -1), (0, 0, 1), (1, 0, -1), (1, 0, 1), (0, 2, 0), (1, -1, 0), (1, 1, 0), (1, 0, 2), (2, -1, 0), (2, 1, 0), (2, 0, -1), (2, 0, 1), (3, 0, -1), (3, 0, 1), (2, 2, 0), (3, -1, 0), (3, 1, 0))),
    ((0, 1), ((3, 0, 2), (0, -1, -1), (0, -1, 1), (1, -1, -1), (1, 1, -1))),
    ((-1, 0), ((0, 1, -1), (0, 1, 1), (1, -1, 1), (1, 1, 1))),
    ((1, 0), ((0, 0, 2), (1, 2, 0))),
    ((-1, -1), ((0, 2, -1), (0, 2, 1), (1, -1, 2), (1, 1, 2), (2, -1, -1), (2, -1, 1), (3, -1, -1), (3, 1, -1), (2, 1, -1), (2, 1, 1), (3, -1, 1), (3, 1, 1), (2, 0, 2), (3, 2, 0))),
    ((1, -1), ((2, 2, -1), (2, 2, 1), (3, -1, 2), (3, 1, 2))),
    ((-1, 1), ((0, -1, 2), (1, 2, -1))),
    ((1, 1), ((0, 1, 2), (1, 2, 1), (0, 2, 2), (1, 2, 2))),
    ((0, 2), ((2, -1, 2), (3, 2, -1))),
    ((2, 0), ((2, 1, 2), (3, 2, 1))),
    ((-1, 2), ((2, 2, 2), (3, 2, 2))),
    ((2, -1), ()),
    ((1, 2), ()),
    ((2, 1), ()),
    ((2, 2), ()),
)
FIRST = (0, 1, 0, 1)
SUB = 64
W_SLOTS = (1, 3, 5, 7, 10, 13)
W_EARLY = 3


def kernel(q_hbm, k_hbm, v_hbm, w_hbm, mask_hbm, out_ref, mask_ref, qs, kv, wbuf, abuf, m_ref, acc_ref,
           ysend, yin, total,
           local_sem, kv_send, kv_recv, kv_sib, w_send, wz_recv, wx_recv, wx_sib,
           a_send, a_recv, y_send, y_recv):
    ctx, tp = lax.axis_index("ctx"), lax.axis_index("tp")
    x, zl, core = ctx // 8, (ctx // 2) % 4, ctx % 2
    y, zh = tp // 4, tp % 4
    z = zh * 4 + zl

    def at_x(d):
        return (((x + d + 4) % 4) * 8 + zl * 2 + core, tp)

    def at_z(d):
        zz = (z + d + 16) % 16
        return (x * 8 + (zz % 4) * 2 + core, y * 4 + zz // 4)

    def at_y(d):
        return (ctx, ((y + d + 4) % 4) * 4 + zh)

    devices = {"x+": at_x(1), "x-": at_x(-1), "x2": at_x(2), "z+": at_z(1), "z-": at_z(-1), "z2": at_z(2),
               "back": at_z(-2), "s": (x * 8 + zl * 2 + (1 - core), tp), "y+": at_y(1), "y-": at_y(-1), "y2": at_y(2),
               "h+": at_z(4), "h-": at_z(-4), "f+": at_z(5), "f-": at_z(-5)}

    def remote(src, dst, ssem, rsem, to):
        return pltpu.make_async_remote_copy(src_ref=src, dst_ref=dst, send_sem=ssem, recv_sem=rsem,
                                            device_id=devices[to], device_id_type=MESH)

    def group_of(dx, dz):
        return ((x + dx + 4) % 4) * 4 + (zl + dz + 4) % 4

    own_group = x * 4 + zl

    def load(src, dst, kind):
        pltpu.make_async_copy(src, dst, local_sem.at[kind]).start()

    def loaded(whole, kind):
        pltpu.make_async_copy(whole, whole, local_sem.at[kind]).wait()

    def kv_at(group, which, sub):
        return ((group * 2 + which) * 4 + sub) * 2

    head = pl.ds(pl.multiple_of(y * HDIM, HDIM), HDIM)
    for sub in range(4):
        rows = pl.ds(sub * SUB, SUB)
        load(k_hbm.at[rows, head], kv.at[kv_at(own_group, core, sub)], sub)
        load(v_hbm.at[rows, head], kv.at[kv_at(own_group, core, sub) + 1], sub)
    for b in range(2):
        for h in range(2):
            load(q_hbm.at[pl.ds(b * BLOCK, BLOCK), pl.ds(h * HDIM, HDIM)], qs.at[pl.ds((b * 2 + h) * HDIM, HDIM)], 4)

    def w_columns(yy, zz):
        return pl.ds(pl.multiple_of((yy * 4 + zz) * 512, 512), 512)

    load(mask_hbm, mask_ref, 5)
    for yy in range(4):
        load(w_hbm.at[:, w_columns(yy, zh)], wbuf.at[zh, yy], 6)

    barrier = pltpu.get_barrier_semaphore()
    for device in devices.values():
        pl.semaphore_signal(barrier, inc=1, device_id=device, device_id_type=MESH)
    pl.semaphore_wait(barrier, len(devices))

    shift = {"x+": (-1, 0), "x-": (1, 0), "x2": (2, 0), "z+": (0, -1), "z-": (0, 1), "z2": (0, 2)}
    count = [0]

    def kv_ref(sub, dx, dz, part):
        first = kv_at(group_of(dx, dz), core, sub)
        return kv.at[pl.ds(first, 2)] if part is None else kv.at[pl.ds(first + part, 1)]

    def kv_forward(sub, dx, dz, part, to):
        ref = kv_ref(sub, dx, dz, part)
        count[0] += 2 if part is None else 1
        if to == "s":
            rsem = kv_sib.at[dx % 4, dz % 4]
        else:
            sx, sz = shift[to]
            rsem = kv_recv.at[sub, (dx + sx) % 4, (dz + sz) % 4]
        remote(ref, ref, kv_send, rsem, to).start()

    def kv_handle(sub, dx, dz):
        along = (dx, dz) if FIRST[sub] == 0 else (dz, dx)
        one, two = ("x", "z") if FIRST[sub] == 0 else ("z", "x")
        if (dx, dz) == (0, 0):
            loaded(kv_ref(sub, 0, 0, None), sub)
        else:
            ref = kv_ref(sub, dx, dz, None)
            remote(ref, ref, kv_send, kv_recv.at[sub, dx % 4, dz % 4], "s").wait_recv()
        if along[1] == 0:
            if along[0] == 0:
                kv_forward(sub, dx, dz, None, one + "+")
                kv_forward(sub, dx, dz, None, one + "-")
                kv_forward(sub, dx, dz, None, one + "2")
            kv_forward(sub, dx, dz, None, two + "+")
            kv_forward(sub, dx, dz, None, two + "-")
        elif along[1] == -1:
            kv_forward(sub, dx, dz, 0, two + "+")
        elif along[1] == 1:
            kv_forward(sub, dx, dz, 1, two + "-")
        kv_forward(sub, dx, dz, None, "s")

    row0 = core * 128
    w_dirs = {"+": (1, ((1, 0), (1, 64), (2, 0))), "-": (-1, ((1, 0), (1, 64), (2, 64)))}
    w_pieces = [(name, j) for j in range(3) for name in w_dirs]
    w_index = {piece: n for n, piece in enumerate(w_pieces)}

    def w_ref(name, j, dx, part=None, own=False, other=False):
        sign, pieces = w_dirs[name]
        reach, first = pieces[j]
        rows, size = ((1 - core) * 128 if other else row0) + first, 64
        if part is not None:
            rows, size = rows + part * 32, 32
        source = zh if own else (zh - sign * reach + 4) % 4
        return wbuf.at[source, (x + dx + 4) % 4, pl.ds(pl.multiple_of(rows, 32), size)]

    def w_first():
        for name, j in w_pieces:
            sign, pieces = w_dirs[name]
            reach, first = pieces[j]

            @pl.when(zl == (3 if sign == 1 else 0))
            def _():
                src = w_hbm.at[pl.ds(pl.multiple_of(row0 + first, 64), 64), w_columns(x, (zh + sign * reach + 4) % 4)]
                remote(src, w_ref(name, j, 0, own=True), w_send, wz_recv.at[w_index[name, j]],
                       ("z" if reach == 1 else "f") + name).start()

    def w_place(name, number):
        return zl == (number if name == "+" else 3 - number)

    def w_slot(s, then=False):
        for name, j in w_pieces:
            number = s - j
            if 0 <= number <= 3:
                @pl.when(w_place(name, number))
                def _():
                    ref = w_ref(name, j, 0)
                    copy = remote(ref, ref, w_send, wz_recv.at[w_index[name, j]], "z" + name)
                    copy.wait_recv()
                    if number < 3:
                        copy.start()
                    if then:
                        w_x1(name, j)

    def w_x1_copy(name, j, to):
        ref = w_ref(name, j, 0)
        n = w_index[name, j]
        rsem = wx_sib if to == "s" else wx_recv.at[n, shift[to][0] % 4 - 1]
        return remote(ref, ref, w_send, rsem, to)

    def w_x1(name, j):
        for to in ("x+", "x-", "s"):
            w_x1_copy(name, j, to).start()

    def w_x1_early():
        for name, j in w_pieces:
            numbers = [number for number in range(4) if number + j < W_EARLY]
            if len(numbers) == 4:
                w_x1(name, j)
            elif numbers:
                @pl.when(zl < len(numbers) if name == "+" else zl > 3 - len(numbers))
                def _():
                    w_x1(name, j)

    def w_forward(name, j, dx, part, to):
        ref = w_ref(name, j, dx, part)
        n = w_index[name, j]
        rsem = wx_sib if to == "s" else wx_recv.at[n, (dx + shift[to][0]) % 4 - 1]
        remote(ref, ref, w_send, rsem, to).start()

    def w_wait(name, j, dx):
        ref = w_ref(name, j, dx)
        remote(ref, ref, w_send, wx_recv.at[w_index[name, j], dx % 4 - 1], "s").wait_recv()

    def w_x2(name, j):
        w_wait(name, j, -1)
        w_forward(name, j, -1, 0, "x+")
        w_wait(name, j, 1)
        w_forward(name, j, 1, 1, "x-")
        w_forward(name, j, -1, None, "s")
        w_forward(name, j, 1, None, "s")

    def w_x3(name, j):
        w_wait(name, j, 2)
        w_forward(name, j, 2, None, "s")

    def w_x4():
        ref = wbuf.at[pl.ds(0, 3), pl.ds(0, 2)]
        remote(ref, ref, w_send, wx_sib, "s").wait_recv()

    m_ref[...] = jnp.full(m_ref.shape, -1e30, F32)
    acc_ref[...] = jnp.zeros(acc_ref.shape, F32)
    loaded(mask_ref, 5)
    loaded(qs, 4)
    ones = jnp.ones((512, HDIM), BF16)

    def attend(group):
        both = kv[pl.ds(group * 16, 16)].reshape(8, 2, SUB, HDIM)
        keys = both[:, 0].reshape(512, HDIM)
        values = jnp.concatenate([both[:, 1].reshape(512, HDIM), ones], axis=1)
        bias = [[(mask_ref[ctx * 2 + b, group * 4 + j].astype(F32) - 1.0) * 1e30 for j in range(4)] for b in range(2)]
        scores = [lax.dot_general(qs[n * 256:(n + 1) * 256], keys, (((1,), (1,)), ((), ())), preferred_element_type=F32)
                  for n in range(2)]
        for n in range(2):
            rows = slice(n * 256, (n + 1) * 256)
            parts = [scores[n][:, j * BLOCK:(j + 1) * BLOCK] * SCALE2 + bias[n * 256 // 256][j] for j in range(4)]
            top = jnp.maximum(jnp.maximum(parts[0], parts[1]), jnp.maximum(parts[2], parts[3]))
            old = m_ref[rows]
            new = jnp.maximum(old, jnp.max(top, axis=1, keepdims=True))
            factor = jnp.exp2(old - new)
            weights = jnp.concatenate([jnp.exp2(part - new).astype(BF16) for part in parts], axis=1)
            m_ref[rows] = new
            acc_ref[rows] = acc_ref[rows] * jnp.concatenate([factor, factor], axis=1) + jnp.dot(
                weights, values, preferred_element_type=F32)

    def pick(number, axis):
        value = 0
        for e, (offset, _) in enumerate(PROGRAM):
            if offset[axis] % 4:
                value = value + jnp.where(number == e, offset[axis] % 4, 0)
        return value

    for sub in range(4):
        kv_handle(sub, 0, 0)
    w_first()

    def step(i, carry):
        for e, (_, pieces) in enumerate(PROGRAM):
            if pieces or e in W_SLOTS:
                @pl.when(i == e)
                def _():
                    for piece in pieces:
                        kv_handle(*piece)
                    if e in W_SLOTS:
                        if W_SLOTS.index(e) == W_EARLY:
                            w_x1_early()
                        w_slot(W_SLOTS.index(e), then=W_SLOTS.index(e) >= W_EARLY)

        dx, dz = pick(i, 0), pick(i, 1)
        group = ((x + dx) % 4) * 4 + (zl + dz) % 4
        ref = kv.at[pl.ds(kv_at(group, 1 - core, 0), 8)]
        remote(ref, ref, kv_send, kv_sib.at[dx, dz], "s").wait_recv()

        @pl.when(group <= own_group)
        def _():
            attend(group)
        return carry

    lax.fori_loop(0, len(PROGRAM), step, 0)

    def a_ref(dzh, quarter, part):
        rows = (quarter % 2) * 64
        ref = abuf.at[(zh + dzh + 4) % 4, quarter // 2]
        return ref.at[pl.ds(rows, 64)] if part is None else ref.at[pl.ds(rows + part * 32, 32)]

    def a_forward(dzh, quarter, part, to):
        ref = a_ref(dzh, quarter, part)
        there = dzh - 1 if to == "h+" else dzh + 1
        remote(ref, ref, a_send, a_recv.at[quarter, there % 4 - 1], to).start()

    def a_wait(dzh, quarter):
        ref = a_ref(dzh, quarter, None)
        remote(ref, ref, a_send, a_recv.at[quarter, dzh % 4 - 1], "s").wait_recv()

    def a_direct(quarter):
        a_forward(0, quarter, None, "h+")
        a_forward(0, quarter, None, "h-")

    def a_relay(quarter):
        a_wait(-1, quarter)
        a_forward(-1, quarter, 0, "h+")
        a_wait(1, quarter)
        a_forward(1, quarter, 1, "h-")

    for b in range(2):
        rows = pl.ds(b * 256, 256)
        done = (acc_ref[rows, :HDIM] / acc_ref[rows, HDIM:]).astype(BF16)
        abuf[zh, b] = jnp.concatenate([done[:BLOCK], done[BLOCK:]], axis=1)
        a_direct(2 * b)
        a_direct(2 * b + 1)

    def project(dzh, half=None):
        zz = (zh + dzh + 4) % 4
        rows = slice(None) if half is None else slice(half * 128, half * 128 + 128)
        attended = abuf[zz].reshape(256, 256) if half is None else abuf[zz, half]
        for dy in range(4):
            part = jnp.dot(attended, wbuf[zz, (y + dy) % 4], preferred_element_type=F32)
            total[dy, rows] = part if half is None else total[dy, rows] + part

    def y_partial(half):
        a_wait(2, 2 * half)
        a_wait(2, 2 * half + 1)
        zz = (zh + 2) % 4
        rows = slice(half * 128, half * 128 + 128)
        for n, (dy, to) in enumerate(((2, "y2"), (1, "y+"), (3, "y-"), (0, None))):
            part = total[dy, rows] + jnp.dot(abuf[zz, half], wbuf[zz, (y + dy) % 4], preferred_element_type=F32)
            if to is None:
                total[dy, rows] = part
            else:
                ysend[half, n] = part.astype(BF16)
                remote(ysend.at[half, n], yin.at[half, n], y_send, y_recv.at[half, n], to).start()

    def y_sum(half):
        rows = slice(half * 128, half * 128 + 128)
        result = total[0, rows]
        for n in range(3):
            remote(ysend.at[half, n], yin.at[half, n], y_send, y_recv.at[half, n], "s").wait_recv()
            result = result + yin[half, n].astype(F32)
        out_ref[rows] = result.astype(BF16)

    def each(action, j):
        for name in w_dirs:
            action(name, j)

    loaded(wbuf.at[zh], 6)
    project(0)
    each(w_x2, 0)
    each(w_x2, 1)
    a_relay(0)
    each(w_x2, 2)
    a_relay(1)
    each(w_x3, 0)
    a_relay(2)
    each(w_x3, 1)
    each(w_x3, 2)
    a_relay(3)
    w_x4()
    for half in range(2):
        project(-1, half)
        project(1, half)
        y_partial(half)
    y_sum(0)
    y_sum(1)

    for sent, sem in ((kv.at[pl.ds(0, count[0])], kv_send), (wbuf.at[pl.ds(0, 3)], w_send),
                      (abuf.at[pl.ds(0, 3)], a_send), (ysend, y_send)):
        remote(sent, sent, sem, kv_recv.at[0, 0, 0], "s").wait_send()


def body(queries, keys, values, out_weight, storm_mask):
    rows, width = queries.shape
    anywhere = pl.BlockSpec(memory_space=pl.ANY)
    dma = pltpu.SemaphoreType.DMA
    return pl.pallas_call(
        kernel,
        out_shape=jax.ShapeDtypeStruct((rows, 512), BF16),
        in_specs=[anywhere, anywhere, anywhere, anywhere, anywhere],
        out_specs=pl.BlockSpec(memory_space=pltpu.VMEM),
        scratch_shapes=[
            pltpu.SMEM(storm_mask.shape, jnp.int32),
            pltpu.VMEM((512, HDIM), BF16),
            pltpu.VMEM((256, SUB, HDIM), BF16),
            pltpu.VMEM((4, 4, 256, 512), BF16),
            pltpu.VMEM((4, 2, BLOCK, 256), BF16),
            pltpu.VMEM((512, HDIM), F32),
            pltpu.VMEM((512, 256), F32),
            pltpu.VMEM((2, 3, BLOCK, 512), BF16),
            pltpu.VMEM((2, 3, BLOCK, 512), BF16),
            pltpu.VMEM((4, 256, 512), F32),
            dma((7,)), dma, dma((4, 4, 4)), dma((4, 4)),
            dma, dma((6,)), dma((6, 3)), dma,
            dma, dma((4, 3)), dma, dma((2, 3)),
        ],
        compiler_params=pltpu.CompilerParams(
            collective_id=0, has_side_effects=True, vmem_limit_bytes=56 * 1024 * 1024),
    )(queries, keys, values, out_weight, storm_mask)


def solution(mesh):
    placed = (P("ctx", "tp"), P("ctx", None), P("ctx", None), P("tp", None), P())
    return jax.shard_map(
        body, mesh=mesh, in_specs=placed, out_specs=P("ctx", "tp"), check_vma=False
    )
```

```python
import functools

import jax
import jax.numpy as jnp
from jax import lax
from jax.experimental import pallas as pl
from jax.experimental.pallas import tpu as pltpu
from jax.sharding import PartitionSpec as P

HDIM = 128
BLOCK = 128
MESH = pl.DeviceIdType.MESH
F32 = jnp.float32
BF16 = jnp.bfloat16
SCALE2 = HDIM ** (-0.5) * 1.4426950408889634
PROGRAM = (
    ((0, 0), ()),
    ((0, -1), ((0, -1, 0), (0, 1, 0), (0, 0, -1), (0, 0, 1), (1, 0, -1), (1, 0, 1), (0, 2, 0), (1, -1, 0), (1, 1, 0), (1, 0, 2), (2, -1, 0), (2, 1, 0), (2, 0, -1), (2, 0, 1), (3, 0, -1), (3, 0, 1), (2, 2, 0), (3, -1, 0), (3, 1, 0))),
    ((0, 1), ((3, 0, 2), (0, -1, -1), (0, -1, 1), (1, -1, -1), (1, 1, -1))),
    ((-1, 0), ((0, 1, -1), (0, 1, 1), (1, -1, 1), (1, 1, 1))),
    ((1, 0), ((0, 0, 2), (1, 2, 0))),
    ((-1, -1), ((0, 2, -1), (0, 2, 1), (1, -1, 2), (1, 1, 2), (2, -1, -1), (2, -1, 1), (3, -1, -1), (3, 1, -1), (2, 1, -1), (2, 1, 1), (3, -1, 1), (3, 1, 1), (2, 0, 2), (3, 2, 0))),
    ((1, -1), ((2, 2, -1), (2, 2, 1), (3, -1, 2), (3, 1, 2))),
    ((-1, 1), ((0, -1, 2), (1, 2, -1))),
    ((1, 1), ((0, 1, 2), (1, 2, 1), (0, 2, 2), (1, 2, 2))),
    ((0, 2), ((2, -1, 2), (3, 2, -1))),
    ((2, 0), ((2, 1, 2), (3, 2, 1))),
    ((-1, 2), ((2, 2, 2), (3, 2, 2))),
    ((2, -1), ()),
    ((1, 2), ()),
    ((2, 1), ()),
    ((2, 2), ()),
)
FIRST = (0, 1, 0, 1)
SUB = 64
W_SLOTS = (1, 3, 5, 7, 10, 13)
W_ACROSS = (14, 15)
W_EARLY = 3


def kernel(q_hbm, k_hbm, v_hbm, w_hbm, mask_hbm, out_ref, mask_ref, qs, kv, wbuf, abuf, m_ref, acc_ref,
           ysend, yin, total,
           local_sem, kv_send, kv_recv, kv_sib, w_send, wz_recv, wx_recv, wx_sib,
           a_send, a_recv, y_send, y_recv):
    ctx, tp = lax.axis_index("ctx"), lax.axis_index("tp")
    x, zl, core = ctx // 8, (ctx // 2) % 4, ctx % 2
    y, zh = tp // 4, tp % 4
    z = zh * 4 + zl

    def at_x(d):
        return (((x + d + 4) % 4) * 8 + zl * 2 + core, tp)

    def at_z(d):
        zz = (z + d + 16) % 16
        return (x * 8 + (zz % 4) * 2 + core, y * 4 + zz // 4)

    def at_y(d):
        return (ctx, ((y + d + 4) % 4) * 4 + zh)

    devices = {"x+": at_x(1), "x-": at_x(-1), "x2": at_x(2), "z+": at_z(1), "z-": at_z(-1), "z2": at_z(2),
               "back": at_z(-2), "s": (x * 8 + zl * 2 + (1 - core), tp), "y+": at_y(1), "y-": at_y(-1), "y2": at_y(2),
               "h+": at_z(4), "h-": at_z(-4), "f+": at_z(5), "f-": at_z(-5)}

    def remote(src, dst, ssem, rsem, to):
        return pltpu.make_async_remote_copy(src_ref=src, dst_ref=dst, send_sem=ssem, recv_sem=rsem,
                                            device_id=devices[to], device_id_type=MESH)

    def group_of(dx, dz):
        return ((x + dx + 4) % 4) * 4 + (zl + dz + 4) % 4

    own_group = x * 4 + zl

    def load(src, dst, kind):
        pltpu.make_async_copy(src, dst, local_sem.at[kind]).start()

    def loaded(whole, kind):
        pltpu.make_async_copy(whole, whole, local_sem.at[kind]).wait()

    def kv_at(group, which, sub):
        return ((group * 2 + which) * 4 + sub) * 2

    head = pl.ds(pl.multiple_of(y * HDIM, HDIM), HDIM)
    for sub in range(4):
        rows = pl.ds(sub * SUB, SUB)
        load(k_hbm.at[rows, head], kv.at[kv_at(own_group, core, sub)], sub)
        load(v_hbm.at[rows, head], kv.at[kv_at(own_group, core, sub) + 1], sub)
    for b in range(2):
        for h in range(2):
            load(q_hbm.at[pl.ds(b * BLOCK, BLOCK), pl.ds(h * HDIM, HDIM)], qs.at[pl.ds((b * 2 + h) * HDIM, HDIM)], 4)

    def w_columns(yy, zz):
        return pl.ds(pl.multiple_of((yy * 4 + zz) * 512, 512), 512)

    load(mask_hbm, mask_ref, 5)
    for yy in range(4):
        load(w_hbm.at[:, w_columns(yy, zh)], wbuf.at[zh, yy], 6)

    barrier = pltpu.get_barrier_semaphore()
    for device in devices.values():
        pl.semaphore_signal(barrier, inc=1, device_id=device, device_id_type=MESH)
    pl.semaphore_wait(barrier, len(devices))

    shift = {"x+": (-1, 0), "x-": (1, 0), "x2": (2, 0), "z+": (0, -1), "z-": (0, 1), "z2": (0, 2)}
    count = [0] * 4

    def at(places, action):
        if len(places) == 4:
            action()
        elif places:
            here = x == places[0]
            for place in places[1:]:
                here = here | (x == place)
            pl.when(here)(action)

    def kv_ref(sub, dx, dz, part):
        first = kv_at(group_of(dx, dz), core, sub)
        return kv.at[pl.ds(first, 2)] if part is None else kv.at[pl.ds(first + part, 1)]

    def kv_forward(sub, dx, dz, part, to):
        ref = kv_ref(sub, dx, dz, part)
        if to == "s":
            rsem = kv_sib.at[dx % 4, dz % 4]
        else:
            sx, sz = shift[to]
            rsem = kv_recv.at[sub, (dx + sx) % 4, (dz + sz) % 4]
        remote(ref, ref, kv_send, rsem, to).start()

    def kv_handle(sub, dx, dz):
        along = (dx, dz) if FIRST[sub] == 0 else (dz, dx)
        one, two = ("x", "z") if FIRST[sub] == 0 else ("z", "x")
        wanted = [v for v in range(4) if (v + dx) % 4 <= v]
        held = sorted(set(wanted) | ({0} if FIRST[sub] == 1 and dx == 1 else set()))
        forwards = []

        def forward(part, to):
            places = wanted
            if to[0] == "x":
                move = {"+": 1, "-": -1, "2": 2}[to[1]]
                places = [v for v in held if (v + dx) % 4 <= (v + move) % 4
                          or (v == 1 and dx == 0 and move == -1 and FIRST[sub] == 1)]
            for v in places:
                count[v] += 2 if part is None else 1
            if forwards and forwards[-1][0] == places:
                forwards[-1][1].append((part, to))
            else:
                forwards.append((places, [(part, to)]))

        def arrive():
            ref = kv_ref(sub, dx, dz, None)
            if (dx, dz) == (0, 0):
                loaded(ref, sub)
            else:
                remote(ref, ref, kv_send, kv_recv.at[sub, dx % 4, dz % 4], "s").wait_recv()

        if along[1] == 0:
            if along[0] == 0:
                for sign in "+-2":
                    forward(None, one + sign)
            forward(None, two + "+")
            forward(None, two + "-")
        elif along[1] == -1:
            forward(0, two + "+")
        elif along[1] == 1:
            forward(1, two + "-")
        forward(None, "s")
        at(held, arrive)
        for places, which in forwards:
            def start():
                for part, to in which:
                    kv_forward(sub, dx, dz, part, to)

            at(places, start)

    row0 = core * 128
    w_dirs = {"+": (1, ((1, 0), (1, 64), (2, 0))), "-": (-1, ((1, 0), (1, 64), (2, 64)))}
    w_pieces = [(name, j) for j in range(3) for name in w_dirs]
    w_index = {piece: n for n, piece in enumerate(w_pieces)}

    def w_ref(name, j, dx, part=None, own=False, other=False):
        sign, pieces = w_dirs[name]
        reach, first = pieces[j]
        rows, size = ((1 - core) * 128 if other else row0) + first, 64
        if part is not None:
            rows, size = rows + part * 32, 32
        source = zh if own else (zh - sign * reach + 4) % 4
        return wbuf.at[source, (x + dx + 4) % 4, pl.ds(pl.multiple_of(rows, 32), size)]

    def w_first():
        for name, j in w_pieces:
            sign, pieces = w_dirs[name]
            reach, first = pieces[j]

            @pl.when(zl == (3 if sign == 1 else 0))
            def _():
                src = w_hbm.at[pl.ds(pl.multiple_of(row0 + first, 64), 64), w_columns(x, (zh + sign * reach + 4) % 4)]
                remote(src, w_ref(name, j, 0, own=True), w_send, wz_recv.at[w_index[name, j]],
                       ("z" if reach == 1 else "f") + name).start()

    def w_place(name, number):
        return zl == (number if name == "+" else 3 - number)

    def w_slot(s, then=False):
        for name, j in w_pieces:
            number = s - j
            if 0 <= number <= 3:
                @pl.when(w_place(name, number))
                def _():
                    ref = w_ref(name, j, 0)
                    copy = remote(ref, ref, w_send, wz_recv.at[w_index[name, j]], "z" + name)
                    copy.wait_recv()
                    if number < 3:
                        copy.start()
                    if then:
                        w_x1(name, j)

    def w_x1_copy(name, j, to):
        ref = w_ref(name, j, 0)
        n = w_index[name, j]
        rsem = wx_sib if to == "s" else wx_recv.at[n, shift[to][0] % 4 - 1]
        return remote(ref, ref, w_send, rsem, to)

    def w_x1(name, j):
        for to in ("x+", "x-", "s"):
            w_x1_copy(name, j, to).start()

    def w_x1_early():
        for name, j in w_pieces:
            numbers = [number for number in range(4) if number + j < W_EARLY]
            if len(numbers) == 4:
                w_x1(name, j)
            elif numbers:
                @pl.when(zl < len(numbers) if name == "+" else zl > 3 - len(numbers))
                def _():
                    w_x1(name, j)

    def w_forward(name, j, dx, part, to):
        ref = w_ref(name, j, dx, part)
        n = w_index[name, j]
        rsem = wx_sib if to == "s" else wx_recv.at[n, (dx + shift[to][0]) % 4 - 1]
        remote(ref, ref, w_send, rsem, to).start()

    def w_wait(name, j, dx):
        ref = w_ref(name, j, dx)
        remote(ref, ref, w_send, wx_recv.at[w_index[name, j], dx % 4 - 1], "s").wait_recv()

    def w_x2(name, j):
        w_wait(name, j, -1)
        w_forward(name, j, -1, 0, "x+")
        w_wait(name, j, 1)
        w_forward(name, j, 1, 1, "x-")
        w_forward(name, j, -1, None, "s")
        w_forward(name, j, 1, None, "s")

    def w_x3(name, j):
        w_wait(name, j, 2)
        w_forward(name, j, 2, None, "s")

    def w_x4():
        ref = wbuf.at[pl.ds(0, 3), pl.ds(0, 2)]
        remote(ref, ref, w_send, wx_sib, "s").wait_recv()

    def each(action, j):
        for name in w_dirs:
            action(name, j)

    m_ref[...] = jnp.full(m_ref.shape, -1e30, F32)
    acc_ref[...] = jnp.zeros(acc_ref.shape, F32)
    loaded(mask_ref, 5)
    loaded(qs, 4)
    ones = jnp.ones((512, HDIM), BF16)

    def attend(group):
        both = kv[pl.ds(group * 16, 16)].reshape(8, 2, SUB, HDIM)
        keys = both[:, 0].reshape(512, HDIM)
        values = jnp.concatenate([both[:, 1].reshape(512, HDIM), ones], axis=1)
        bias = [[(mask_ref[ctx * 2 + b, group * 4 + j].astype(F32) - 1.0) * 1e30 for j in range(4)] for b in range(2)]
        scores = [lax.dot_general(qs[n * 256:(n + 1) * 256], keys, (((1,), (1,)), ((), ())), preferred_element_type=F32)
                  for n in range(2)]
        for n in range(2):
            rows = slice(n * 256, (n + 1) * 256)
            parts = [scores[n][:, j * BLOCK:(j + 1) * BLOCK] * SCALE2 + bias[n * 256 // 256][j] for j in range(4)]
            top = jnp.maximum(jnp.maximum(parts[0], parts[1]), jnp.maximum(parts[2], parts[3]))
            old = m_ref[rows]
            new = jnp.maximum(old, jnp.max(top, axis=1, keepdims=True))
            factor = jnp.exp2(old - new)
            weights = jnp.concatenate([jnp.exp2(part - new).astype(BF16) for part in parts], axis=1)
            m_ref[rows] = new
            acc_ref[rows] = acc_ref[rows] * jnp.concatenate([factor, factor], axis=1) + jnp.dot(
                weights, values, preferred_element_type=F32)

    def pick(number, axis):
        value = 0
        for e, (offset, _) in enumerate(PROGRAM):
            if offset[axis] % 4:
                value = value + jnp.where(number == e, offset[axis] % 4, 0)
        return value

    w_first()
    for sub in range(4):
        kv_handle(sub, 0, 0)

    def step(i, carry):
        for e, (_, pieces) in enumerate(PROGRAM):
            if pieces or e in W_SLOTS or e in W_ACROSS:
                @pl.when(i == e)
                def _():
                    for piece in pieces:
                        kv_handle(*piece)
                    if e in W_SLOTS:
                        if W_SLOTS.index(e) == W_EARLY:
                            w_x1_early()
                        w_slot(W_SLOTS.index(e), then=W_SLOTS.index(e) >= W_EARLY)
                    if e in W_ACROSS:
                        each(w_x2, W_ACROSS.index(e))

        dx, dz = pick(i, 0), pick(i, 1)
        group = ((x + dx) % 4) * 4 + (zl + dz) % 4

        @pl.when((x + dx) % 4 <= x)
        def _():
            ref = kv.at[pl.ds(kv_at(group, 1 - core, 0), 8)]
            remote(ref, ref, kv_send, kv_sib.at[dx, dz], "s").wait_recv()

        @pl.when(group <= own_group)
        def _():
            attend(group)
        return carry

    lax.fori_loop(0, len(PROGRAM), step, 0)

    def a_ref(dzh, quarter, part):
        rows = (quarter % 2) * 64
        ref = abuf.at[(zh + dzh + 4) % 4, quarter // 2]
        return ref.at[pl.ds(rows, 64)] if part is None else ref.at[pl.ds(rows + part * 32, 32)]

    def a_forward(dzh, quarter, part, to):
        ref = a_ref(dzh, quarter, part)
        there = dzh - 1 if to == "h+" else dzh + 1
        remote(ref, ref, a_send, a_recv.at[quarter, there % 4 - 1], to).start()

    def a_wait(dzh, quarter):
        ref = a_ref(dzh, quarter, None)
        remote(ref, ref, a_send, a_recv.at[quarter, dzh % 4 - 1], "s").wait_recv()

    def a_direct(quarter):
        a_forward(0, quarter, None, "h+")
        a_forward(0, quarter, None, "h-")

    def a_relay(quarter):
        a_wait(-1, quarter)
        a_forward(-1, quarter, 0, "h+")
        a_wait(1, quarter)
        a_forward(1, quarter, 1, "h-")

    for b in range(2):
        rows = pl.ds(b * 256, 256)
        done = (acc_ref[rows, :HDIM] / acc_ref[rows, HDIM:]).astype(BF16)
        abuf[zh, b] = jnp.concatenate([done[:BLOCK], done[BLOCK:]], axis=1)
        a_direct(2 * b)
        a_direct(2 * b + 1)

    def project(dzh, half=None):
        zz = (zh + dzh + 4) % 4
        rows = slice(None) if half is None else slice(half * 128, half * 128 + 128)
        attended = abuf[zz].reshape(256, 256) if half is None else abuf[zz, half]
        for dy in range(4):
            part = jnp.dot(attended, wbuf[zz, (y + dy) % 4], preferred_element_type=F32)
            total[dy, rows] = part if half is None else total[dy, rows] + part

    def y_partial(half):
        a_wait(2, 2 * half)
        a_wait(2, 2 * half + 1)
        zz = (zh + 2) % 4
        rows = slice(half * 128, half * 128 + 128)
        for n, (dy, to) in enumerate(((2, "y2"), (1, "y+"), (3, "y-"), (0, None))):
            part = total[dy, rows] + jnp.dot(abuf[zz, half], wbuf[zz, (y + dy) % 4], preferred_element_type=F32)
            if to is None:
                total[dy, rows] = part
            else:
                ysend[half, n] = part.astype(BF16)
                remote(ysend.at[half, n], yin.at[half, n], y_send, y_recv.at[half, n], to).start()

    def y_sum(half):
        rows = slice(half * 128, half * 128 + 128)
        result = total[0, rows]
        for n in range(3):
            remote(ysend.at[half, n], yin.at[half, n], y_send, y_recv.at[half, n], "s").wait_recv()
            result = result + yin[half, n].astype(F32)
        out_ref[rows] = result.astype(BF16)

    loaded(wbuf.at[zh], 6)
    project(0)
    each(w_x2, 2)
    each(w_x3, 0)
    a_relay(0)
    each(w_x3, 1)
    a_relay(1)
    each(w_x3, 2)
    a_relay(2)
    a_relay(3)
    w_x4()
    for half in range(2):
        project(-1, half)
        project(1, half)
        y_partial(half)
    y_sum(0)
    y_sum(1)

    for v in range(4):
        def sent_kv():
            sent = kv.at[pl.ds(0, count[v])]
            remote(sent, sent, kv_send, kv_recv.at[0, 0, 0], "s").wait_send()

        at([v], sent_kv)
    for sent, sem in ((wbuf.at[pl.ds(0, 3)], w_send),
                      (abuf.at[pl.ds(0, 3)], a_send), (ysend, y_send)):
        remote(sent, sent, sem, kv_recv.at[0, 0, 0], "s").wait_send()


def body(queries, keys, values, out_weight, storm_mask):
    rows, width = queries.shape
    anywhere = pl.BlockSpec(memory_space=pl.ANY)
    dma = pltpu.SemaphoreType.DMA
    return pl.pallas_call(
        kernel,
        out_shape=jax.ShapeDtypeStruct((rows, 512), BF16),
        in_specs=[anywhere, anywhere, anywhere, anywhere, anywhere],
        out_specs=pl.BlockSpec(memory_space=pltpu.VMEM),
        scratch_shapes=[
            pltpu.SMEM(storm_mask.shape, jnp.int32),
            pltpu.VMEM((512, HDIM), BF16),
            pltpu.VMEM((256, SUB, HDIM), BF16),
            pltpu.VMEM((4, 4, 256, 512), BF16),
            pltpu.VMEM((4, 2, BLOCK, 256), BF16),
            pltpu.VMEM((512, HDIM), F32),
            pltpu.VMEM((512, 256), F32),
            pltpu.VMEM((2, 3, BLOCK, 512), BF16),
            pltpu.VMEM((2, 3, BLOCK, 512), BF16),
            pltpu.VMEM((4, 256, 512), F32),
            dma((7,)), dma, dma((4, 4, 4)), dma((4, 4)),
            dma, dma((6,)), dma((6, 3)), dma,
            dma, dma((4, 3)), dma, dma((2, 3)),
        ],
        compiler_params=pltpu.CompilerParams(
            collective_id=0, has_side_effects=True, vmem_limit_bytes=56 * 1024 * 1024),
    )(queries, keys, values, out_weight, storm_mask)


def solution(mesh):
    placed = (P("ctx", "tp"), P("ctx", None), P("ctx", None), P("tp", None), P())
    return jax.shard_map(
        body, mesh=mesh, in_specs=placed, out_specs=P("ctx", "tp"), check_vma=False
    )
```
